32 devices in a mesh: parts: 2 (over y), pool: 4 (over z), tp: 4 (over x, core).
Axes of the slice: x: 2, y: 2, z: 4, core: 2. Of those that a mesh axis runs over, the one named last changes fastest.
Arguments:
- queries: bfloat16 [4096, 8192], P(('parts', 'pool'), 'tp'), parts along dimension 0, may hold values from -400 to 400
- suffix_kv: bfloat16 [2, 8, 4096, 128], P(None, 'tp', ('parts', 'pool')), parts along dimension 2, may hold values from -12 to 12
- pool_kv: bfloat16 [2, 8, 64, 128, 128], P(None, 'tp', ('parts', 'pool')), parts along dimension 2, may hold values from -6 to 6
- prefix_pages: int32 [8], P('parts'), parts along dimension 0, may hold values from 1 to 4, as said below
- owner_start: int32 [8], P('parts'), parts along dimension 0, may hold values from 0 to 3
- page_slot: int32 [8, 4, 2], P('parts'), parts along dimension 0, may hold values from 0 to 7, as said below
Outputs:
- attention: bfloat16 [4096, 8192], P(('parts', 'pool'), 'tp'), parts along dimension 0
- new_pool: bfloat16 [2, 8, 64, 128, 128], P(None, 'tp', ('parts', 'pool')), parts along dimension 2
The draws below stay inside these ranges and needn't reach their ends.
There are 2 independent parts, one for each index of `parts`. The reference program is written for one: setup_inputs(seed, part) draws one part's arguments, and reference() takes and returns one part's arrays. A program takes and returns all parts, laid end to end along the dimension named above; each array names one. Nothing has to cross between parts.
Inputs may be any that keep to these rules, and one draw needn't show every extreme that they name: For each owner o, the entries page_slot[:, o, :] name each of its 8 slots exactly once. `prefix_pages`: among the 4 requests of one serving group, at least one has exactly 4 prefix pages.
All inputs are finite; a program needn't handle non-finite values.
Results may differ from the reference program's by a relative error of at most 0.0035.
Values may be sent and summed in bfloat16 or wider, within the bound.
A program may use at most 128 MiB of HBM per device.

```python
import math
import jax
import jax.numpy as jnp
from jax import lax

KVH = 8
HD = 128
GROUP = 8
PAGE = 128
CAP = 2
SUF = 512
REQS = 4
SLOTS = 8
MAXP = 8
SP = 4
POOL_PAGES = 32
N_POOL = 4


def joint_draw(key):
    base_key = jax.random.fold_in(key, 4242)
    key_query, key_cache = jax.random.split(base_key, 2)
    queries = jnp.clip(2.5 * jax.random.normal(key_query, (REQS * SUF, KVH * GROUP * HD), jnp.float32), -15.0, 15.0)
    cache = jnp.clip(jax.random.normal(key_cache, (2, KVH, REQS * SUF, HD), jnp.float32), -6.0, 6.0)
    return (queries, cache)


def draw_queries(key, part):
    return joint_draw(key)[0].astype(jnp.bfloat16)


def draw_suffix_kv(key, part):
    return joint_draw(key)[1].astype(jnp.bfloat16)


def draw_prefix_pages(key, part):
    length_key, pick_key = jax.random.split(jax.random.fold_in(key, 517))
    longest = MAXP - SP
    lengths = jax.random.randint(length_key, (REQS,), 1, longest + 1, dtype=jnp.int32)
    chosen = jax.random.randint(pick_key, (), 0, REQS, dtype=jnp.int32)
    places = jnp.arange(REQS, dtype=jnp.int32)
    return jnp.where(places == chosen, longest, lengths).astype(jnp.int32)


def owner_order(owner_key):
    return jax.random.permutation(owner_key, REQS * CAP).astype(jnp.int32)


def draw_page_slot(key, part):
    owner_keys = jax.random.split(jax.random.fold_in(key, 99), N_POOL)
    orders = jax.vmap(owner_order)(owner_keys).reshape(N_POOL, REQS, CAP)
    return jnp.transpose(orders, (1, 0, 2)).astype(jnp.int32)


def plant(array, rng, low, top_value):
    spot = [jax.random.randint(jax.random.fold_in(rng, axis), (), 0, length) for axis, length in enumerate(array.shape)]
    main_axis = array.shape.index(max(array.shape))
    neighbour = spot[:main_axis] + [(spot[main_axis] + 1) % array.shape[main_axis]] + spot[main_axis + 1:]
    return array.at[tuple(spot)].set(low).at[tuple(neighbour)].set(top_value)


def block_scale(rng, extent, cuts, smallest, largest):
    def one(position, parts):
        steps = jax.random.uniform(jax.random.fold_in(jax.random.fold_in(rng, 6), position), (parts,), jnp.float32, smallest / len(cuts), largest / len(cuts))
        return jnp.repeat(jnp.exp(steps), extent[position] // parts).reshape((-1,) + (1,) * (len(extent) - position - 1))

    gain = one(*cuts[0])
    for cut in cuts[1:]:
        gain = gain * one(*cut)
    return gain


def noise(own_key, extent, width, limit, pieces=(), kind=jnp.bfloat16):
    result = width * jax.random.normal(own_key, extent, jnp.float32)
    if pieces:
        result = result * block_scale(own_key, extent, pieces, -0.22, 0.18)
    return jnp.clip(result, -limit, limit).astype(kind)


def setup_inputs(seed: int = 0, part: int = 0) -> dict:
    key_of = jax.random.split(jax.random.key(seed), 7)
    own_keys = jax.random.split(jax.random.fold_in(key_of[6], part), 7)
    queries = draw_queries(jax.random.fold_in(jax.random.fold_in(key_of[6], part), 71), part)
    suffix_kv = draw_suffix_kv(jax.random.fold_in(jax.random.fold_in(key_of[6], part), 71), part)
    pool_kv = noise(own_keys[2], (2, KVH, POOL_PAGES, PAGE, HD), 1.0, 6.0, ((1, 4), (2, 4)))
    prefix_pages = draw_prefix_pages(jax.random.fold_in(jax.random.fold_in(key_of[6], part), 71), part)
    owner_start = plant(jax.random.randint(own_keys[4], (REQS,), 0, N_POOL), jax.random.fold_in(own_keys[4], 1), 0, N_POOL - 1).astype(jnp.int32)
    page_slot = draw_page_slot(jax.random.fold_in(jax.random.fold_in(key_of[6], part), 71), part)
    return dict(queries=queries, suffix_kv=suffix_kv, pool_kv=pool_kv, prefix_pages=prefix_pages, owner_start=owner_start, page_slot=page_slot)


def page_rows(prefix_pages, owner_start, page_slot):
    numbers = jnp.arange(MAXP, dtype=jnp.int32)
    owner_ids = jnp.mod(owner_start[:, None] + numbers[None, :], N_POOL).astype(jnp.int32)
    level_ids = jnp.broadcast_to(numbers[None, :] // N_POOL, owner_ids.shape)
    request_ids = jnp.broadcast_to(jnp.arange(REQS, dtype=jnp.int32)[:, None], owner_ids.shape)
    return (owner_ids * SLOTS + page_slot[request_ids, owner_ids, level_ids]).astype(jnp.int32)

def reference(queries, suffix_kv, pool_kv, prefix_pages, owner_start, page_slot):
    rows_table = page_rows(prefix_pages, owner_start, page_slot)
    score_scale = 1.0 / math.sqrt(HD)
    page_ids = jnp.arange(MAXP * PAGE, dtype=jnp.int32) // PAGE
    causal = lax.broadcasted_iota(jnp.int32, (SUF, SUF), 1) <= lax.broadcasted_iota(jnp.int32, (SUF, SUF), 0)

    def per_request(request):
        gathered = jnp.take(pool_kv, rows_table[request], axis=2)
        prefix_rows = gathered.reshape(2, KVH, MAXP * PAGE, HD)
        own_rows = lax.dynamic_slice_in_dim(suffix_kv, (request * SUF).astype(jnp.int32), SUF, 2)
        context = jnp.concatenate([prefix_rows, own_rows], axis=2)
        query_rows = lax.dynamic_slice_in_dim(queries, (request * SUF).astype(jnp.int32), SUF, 0)
        query_rows = query_rows.reshape(SUF, KVH, GROUP, HD)
        prefix_seen = page_ids < prefix_pages[request]
        visible = jnp.concatenate([jnp.broadcast_to(prefix_seen[None, :], (SUF, MAXP * PAGE)), causal], axis=1)

        def per_head(kv_head):
            pair = lax.dynamic_index_in_dim(context, kv_head, 1, keepdims=False)
            key_rows = pair[0].astype(jnp.float32)
            value_rows = pair[1].astype(jnp.float32)
            heads_query = lax.dynamic_index_in_dim(query_rows, kv_head, 1, keepdims=False).astype(jnp.float32)
            scores = jnp.einsum('qgd,kd->gqk', heads_query, key_rows) * score_scale
            scores = jnp.where(visible[None], scores, -jnp.inf)
            row_max = lax.optimization_barrier(jnp.max(scores, axis=-1, keepdims=True))
            weights = jnp.exp(scores - row_max)
            weight_sum = lax.optimization_barrier(jnp.sum(weights, axis=-1))
            rounded = lax.optimization_barrier(weights.astype(jnp.bfloat16)).astype(jnp.float32)
            mixed_rows = jnp.einsum('gqk,kd->qgd', rounded, value_rows)
            return mixed_rows / jnp.transpose(weight_sum)[:, :, None]
        heads_out = lax.map(per_head, jnp.arange(KVH, dtype=jnp.int32))
        return jnp.transpose(heads_out, (1, 0, 2, 3)).reshape(SUF, KVH * GROUP * HD).astype(jnp.bfloat16)
    attention = lax.map(per_request, jnp.arange(REQS, dtype=jnp.int32)).reshape(REQS * SUF, KVH * GROUP * HD)
    offsets = jnp.arange(SP, dtype=jnp.int32)
    numbers = prefix_pages[:, None] + offsets[None, :]
    owner_ids = jnp.mod(owner_start[:, None] + numbers, N_POOL).astype(jnp.int32)
    request_ids = jnp.broadcast_to(jnp.arange(REQS, dtype=jnp.int32)[:, None], owner_ids.shape)
    targets = owner_ids * SLOTS + page_slot[request_ids, owner_ids, numbers // N_POOL]
    fresh_pages = suffix_kv.reshape(2, KVH, REQS * SP, PAGE, HD)
    new_pool = pool_kv.at[:, :, targets.reshape(-1).astype(jnp.int32)].set(fresh_pages)
    return (attention, new_pool)
```

```python
import functools
import math

import jax
import jax.numpy as jnp
from jax import lax
from jax.experimental import pallas as pl
from jax.experimental.pallas import tpu as pltpu
from jax.sharding import PartitionSpec as P

NT = (((1,), (1,)), ((), ()))
ROWS = 256
KEY_BLOCK = 512


def exchange(
    groups,
    prefix_levels,
    length_hbm,
    start_hbm,
    slot_hbm,
    q_hbm,
    own_hbm,
    pool_hbm,
    out_ref,
    new_ref,
    length_ref,
    start_ref,
    slot_ref,
    q_ref,
    own_ref,
    pool_ref,
    send,
    recv,
    fresh_send,
    fresh,
    own_values,
    page_keys,
    page_values,
    acc,
    top,
    load_sem,
    send_sem,
    recv_sem,
    fresh_send_sem,
    fresh_recv_sem,
    ready,
):
    me = lax.axis_index("pool")
    last = groups - 1
    others = groups - 1

    barrier = pltpu.get_barrier_semaphore()

    def greet(semaphore, device):
        pl.semaphore_signal(
            semaphore, inc=1, device_id={"pool": device}, device_id_type=pl.DeviceIdType.MESH
        )

    @pl.when(me != last)
    def _():
        for step in range(1, groups):
            greet(barrier, lax.rem(me + step, groups))

    sources = (length_hbm, start_hbm, slot_hbm, pool_hbm, own_hbm, q_hbm)
    targets = (length_ref, start_ref, slot_ref, pool_ref, own_ref, q_ref)
    loads = [
        pltpu.make_async_copy(source, target, load_sem.at[i])
        for i, (source, target) in enumerate(zip(sources, targets))
    ]
    for load in loads:
        load.start()

    local_heads = pool_ref.shape[1]
    slot_count = pool_ref.shape[2]
    page_len = pool_ref.shape[3]
    dim = pool_ref.shape[4]
    levels = slot_ref.shape[1]
    suffix = q_ref.shape[0]
    heads = q_ref.shape[1] // dim
    per_kv = heads // local_heads
    suffix_pages = suffix // page_len
    factor = math.log2(math.e) / math.sqrt(dim)
    rows = min(ROWS, suffix)

    def wrap(value):
        return lax.rem(value + groups * (levels + 1), groups)

    def falling(k):
        return last - k - jnp.where(last - k <= me, 1, 0)

    def rising(k):
        return k + jnp.where(k >= me, 1, 0)

    low = me < groups // 2
    swap = groups >= 4

    def partner(k, early):
        down = falling(k)
        if early and swap and k < 2:
            down = falling(1 - k)
        return jnp.where(low, down, rising(k))

    for load in loads[:4]:
        load.wait()
    my_start = start_ref[me]
    my_length = length_ref[me]

    for level in range(prefix_levels):
        for k in range(others):
            send[level * others + k] = pool_ref[:, :, slot_ref[partner(k, level == 0), level, me]]
    loads[4].wait()
    for k in range(others):
        offset = jnp.minimum(wrap(partner(k, False) - my_start - my_length), suffix_pages - 1)
        fresh_send[k] = own_ref[:, :, offset]

    pl.semaphore_wait(barrier, groups - 2 + jnp.where(me == last, 1, 0))

    @pl.when(me == last)
    def _():
        for step in range(1, groups):
            greet(ready, lax.rem(me + step, groups))

    copies = []
    for level in range(prefix_levels):
        for k in range(others):
            if level == 0 and k == (1 if swap else 0):

                @pl.when(low & (me != last))
                def _():
                    pl.semaphore_wait(ready, 1)

            if level == 0 and k == others - 1:

                @pl.when(jnp.logical_not(low) & (me != last))
                def _():
                    pl.semaphore_wait(ready, 1)

            copy = pltpu.make_async_remote_copy(
                src_ref=send.at[level * others + k],
                dst_ref=recv.at[level * groups + me],
                send_sem=send_sem.at[level * others + k],
                recv_sem=recv_sem.at[level * groups + me],
                device_id={"pool": partner(k, level == 0)},
                device_id_type=pl.DeviceIdType.MESH,
            )
            copy.start()
            copies.append(copy)
    fresh_copies = []
    for k in range(others):
        copy = pltpu.make_async_remote_copy(
            src_ref=fresh_send.at[k],
            dst_ref=fresh.at[me],
            send_sem=fresh_send_sem.at[k],
            recv_sem=fresh_recv_sem.at[me],
            device_id={"pool": partner(k, False)},
            device_id_type=pl.DeviceIdType.MESH,
        )
        copy.start()
        fresh_copies.append(copy)

    def arrived(buffer, semaphores, place):
        return pltpu.make_async_remote_copy(
            src_ref=buffer.at[place],
            dst_ref=buffer.at[place],
            send_sem=semaphores.at[place],
            recv_sem=semaphores.at[place],
            device_id={"pool": lax.rem(me + 1, groups)},
            device_id_type=pl.DeviceIdType.MESH,
        )

    for level in range(prefix_levels):
        recv[level * groups + me] = pool_ref[:, :, slot_ref[me, level, me]]
    offset = jnp.minimum(wrap(me - my_start - my_length), suffix_pages - 1)
    fresh[me] = own_ref[:, :, offset]
    for head in range(local_heads):
        own_values[head, :, :dim] = own_ref[1, head].reshape(suffix, dim)
        own_values[head, :, dim:] = jnp.ones((suffix, dim), jnp.bfloat16)

    masks = {}
    for at in range(0, rows, dim):
        masks[at] = lax.broadcasted_iota(jnp.int32, (rows, dim), 1) + at <= lax.broadcasted_iota(
            jnp.int32, (rows, dim), 0
        )

    def own_step(head, carry):
        kv_head = head // per_kv
        columns = pl.ds(pl.multiple_of(head * dim, dim), dim)
        for first in range(0, suffix, rows):
            end = first + rows
            scores = lax.dot_general(
                q_ref[first:end, columns],
                own_ref[0, kv_head, : end // page_len].reshape(end, dim),
                NT,
                preferred_element_type=jnp.float32,
            )
            pieces = []
            for at in range(0, end, dim):
                piece = scores[:, at : at + dim]
                if at + dim > first + 1:
                    piece = jnp.where(masks[at - first], piece, -jnp.inf)
                pieces.append(piece)
            peak = functools.reduce(jnp.maximum, pieces)
            highest = jnp.broadcast_to(jnp.max(peak, axis=1, keepdims=True), (rows, dim))
            weights = jnp.concatenate(
                [jnp.exp2((piece - highest) * factor).astype(jnp.bfloat16) for piece in pieces], axis=1
            )
            acc[head, first:end] = jnp.dot(
                weights, own_values[kv_head, :end], preferred_element_type=jnp.float32
            )
            top[head, first:end] = highest
        return carry

    loads[5].wait()
    lax.fori_loop(0, heads, own_step, 0, unroll=4)

    for level in range(prefix_levels):
        for step in range(1, groups):
            arrived(recv, recv_sem, level * groups + lax.rem(me + step, groups)).wait_recv()

    first_page = my_start
    for level in range(prefix_levels):
        for owner in range(groups):
            place = level * groups + owner
            number = level * groups + wrap(owner - my_start)
            live = number < my_length
            source = jnp.where(live, place, first_page)
            keep = live.astype(jnp.float32)
            span = slice(place * page_len, (place + 1) * page_len)
            for head in range(local_heads):
                page_keys[head, span] = recv[source, 0, head]
                page_values[head, span, :dim] = recv[place, 1, head] * keep.astype(jnp.bfloat16)
                page_values[head, span, dim:] = jnp.full(
                    (page_len, dim), keep, jnp.float32
                ).astype(jnp.bfloat16)

    total = prefix_levels * groups * page_len
    block = min(KEY_BLOCK, total)

    def page_step(head, carry):
        kv_head = head // per_kv
        columns = pl.ds(pl.multiple_of(head * dim, dim), dim)
        for first in range(0, suffix, rows):
            end = first + rows
            mixed = acc[head, first:end]
            highest = top[head, first:end]
            for key_first in range(0, total, block):
                width = min(block, total - key_first)
                scores = lax.dot_general(
                    q_ref[first:end, columns],
                    page_keys[kv_head, key_first : key_first + width],
                    NT,
                    preferred_element_type=jnp.float32,
                )
                risen = jnp.maximum(highest, jnp.max(scores, axis=1, keepdims=True))
                shrink = jnp.exp2((highest - risen) * factor)
                weights = jnp.concatenate(
                    [
                        jnp.exp2((scores[:, at : at + dim] - risen) * factor).astype(jnp.bfloat16)
                        for at in range(0, width, dim)
                    ],
                    axis=1,
                )
                mixed = mixed * jnp.concatenate([shrink, shrink], axis=1) + jnp.dot(
                    weights,
                    page_values[kv_head, key_first : key_first + width],
                    preferred_element_type=jnp.float32,
                )
                highest = risen
            out_ref[first:end, columns] = (mixed[:, :dim] / mixed[:, dim:]).astype(jnp.bfloat16)
        return carry

    lax.fori_loop(0, heads, page_step, 0, unroll=4)

    places = []
    for request in range(groups):
        length = length_ref[request]
        offset = wrap(me - start_ref[request] - length)
        level = jnp.minimum((length + offset) // groups, levels - 1)
        places.append(jnp.where(offset < suffix_pages, slot_ref[request, level, me], slot_count))

    for copy in copies + fresh_copies:
        copy.wait_send()
    for step in range(1, groups):
        arrived(fresh, fresh_recv_sem, lax.rem(me + step, groups)).wait_recv()
    for slot in range(slot_count):
        chosen = jnp.int32(0)
        hit = jnp.bool_(False)
        for request in range(groups):
            match = places[request] == slot
            chosen = jnp.where(match, request, chosen)
            hit = hit | match
        new_ref[:, :, slot] = jnp.where(hit, fresh[chosen], pool_ref[:, :, slot])


def finish(mixed_ref, pages_ref, out_ref, new_ref, sems):
    copies = []
    count = sems.shape[0] // 2
    rows = mixed_ref.shape[0] // count
    for part in range(count):
        span = pl.ds(part * rows, rows)
        copies.append(pltpu.make_async_copy(mixed_ref.at[span], out_ref.at[span], sems.at[part]))
    copies.append(pltpu.make_async_copy(pages_ref, new_ref, sems.at[count]))
    for copy in copies:
        copy.start()
    for copy in copies:
        copy.wait()


def body(queries, suffix_kv, pool_kv, prefix_pages, owner_start, page_slot):
    groups = lax.axis_size("pool")
    _, local_heads, slot_count, page_len, dim = pool_kv.shape
    levels = page_slot.shape[2]
    suffix, width = queries.shape
    heads = width // dim
    suffix_pages = suffix // page_len
    prefix_levels = max(1, -(-(groups * levels - suffix_pages) // groups))
    pages = prefix_levels * groups
    page_shape = (2, local_heads, page_len, dim)
    own_shape = (2, local_heads, suffix_pages, page_len, dim)
    vmem = pl.BlockSpec(memory_space=pltpu.VMEM)
    bf16 = jnp.bfloat16
    anywhere = pl.BlockSpec(memory_space=pl.ANY)
    hbm = pl.BlockSpec(memory_space=pltpu.HBM)
    slots = jnp.transpose(page_slot, (0, 2, 1))
    dma = pltpu.SemaphoreType.DMA
    mixed, new_pages = pl.pallas_call(
        functools.partial(exchange, groups, prefix_levels),
        out_shape=(pltpu.VMEM(queries.shape, bf16), pltpu.VMEM(pool_kv.shape, bf16)),
        in_specs=[hbm] * 6,
        out_specs=(vmem, vmem),
        scratch_shapes=[
            pltpu.SMEM(prefix_pages.shape, jnp.int32),
            pltpu.SMEM(owner_start.shape, jnp.int32),
            pltpu.SMEM(slots.shape, jnp.int32),
            pltpu.VMEM(queries.shape, bf16),
            pltpu.VMEM(own_shape, bf16),
            pltpu.VMEM(pool_kv.shape, bf16),
            pltpu.VMEM((prefix_levels * (groups - 1),) + page_shape, bf16),
            pltpu.VMEM((pages,) + page_shape, bf16),
            pltpu.VMEM((groups - 1,) + page_shape, bf16),
            pltpu.VMEM((groups,) + page_shape, bf16),
            pltpu.VMEM((local_heads, suffix, 2 * dim), bf16),
            pltpu.VMEM((local_heads, pages * page_len, dim), bf16),
            pltpu.VMEM((local_heads, pages * page_len, 2 * dim), bf16),
            pltpu.VMEM((heads, suffix, 2 * dim), jnp.float32),
            pltpu.VMEM((heads, suffix, dim), jnp.float32),
            dma((6,)),
            dma((prefix_levels * (groups - 1),)),
            dma((pages,)),
            dma((groups - 1,)),
            dma((groups,)),
            pltpu.SemaphoreType.REGULAR,
        ],
        compiler_params=pltpu.CompilerParams(
            collective_id=0, has_side_effects=True, vmem_limit_bytes=44 * 1024 * 1024
        ),
    )(
        *(
            pltpu.with_memory_space_constraint(operand, pltpu.HBM)
            for operand in (
                prefix_pages,
                owner_start,
                slots,
                queries,
                suffix_kv.reshape(own_shape),
                pool_kv,
            )
        )
    )
    return pl.pallas_call(
        finish,
        out_shape=(
            jax.ShapeDtypeStruct(queries.shape, bf16),
            jax.ShapeDtypeStruct(pool_kv.shape, bf16),
        ),
        in_specs=[vmem, vmem],
        out_specs=(anywhere, anywhere),
        scratch_shapes=[dma((4,))],
        compiler_params=pltpu.CompilerParams(vmem_limit_bytes=8 * 1024 * 1024),
    )(mixed, new_pages)


def solution(mesh):
    in_specs = (
        P(("parts", "pool"), "tp"),
        P(None, "tp", ("parts", "pool"), None),
        P(None, "tp", ("parts", "pool"), None, None),
        P("parts"),
        P("parts"),
        P("parts", None, None),
    )
    out_specs = (P(("parts", "pool"), "tp"), P(None, "tp", ("parts", "pool"), None, None))
    return jax.shard_map(body, mesh=mesh, in_specs=in_specs, out_specs=out_specs, check_vma=False)
```

```python
import functools
import math

import jax
import jax.numpy as jnp
from jax import lax
from jax.experimental import pallas as pl
from jax.experimental.pallas import tpu as pltpu
from jax.sharding import PartitionSpec as P

NT = (((1,), (1,)), ((), ()))
ROWS = 256
KEY_BLOCK = 512


def exchange(
    groups,
    prefix_levels,
    length_hbm,
    start_hbm,
    slot_hbm,
    q_hbm,
    own_hbm,
    pool_hbm,
    out_ref,
    new_ref,
    length_ref,
    start_ref,
    slot_ref,
    q_ref,
    own_ref,
    pool_ref,
    send,
    recv,
    fresh_send,
    fresh,
    own_values,
    page_keys,
    page_values,
    acc,
    top,
    load_sem,
    send_sem,
    recv_sem,
    fresh_send_sem,
    fresh_recv_sem,
    ready,
):
    me = lax.axis_index("pool")
    last = groups - 1
    others = groups - 1

    barrier = pltpu.get_barrier_semaphore()

    def greet(semaphore, device):
        pl.semaphore_signal(
            semaphore, inc=1, device_id={"pool": device}, device_id_type=pl.DeviceIdType.MESH
        )

    @pl.when(me != last)
    def _():
        for step in range(1, groups):
            greet(barrier, lax.rem(me + step, groups))

    local_heads = pool_ref.shape[1]
    pairs = [(length_hbm, length_ref), (start_hbm, start_ref), (slot_hbm, slot_ref)]
    for kind in range(2):
        for head in range(local_heads):
            pairs.append((pool_hbm.at[kind, head], pool_ref.at[kind, head]))
    pairs += [(own_hbm, own_ref), (q_hbm, q_ref)]
    loads = [
        pltpu.make_async_copy(source, target, load_sem.at[i])
        for i, (source, target) in enumerate(pairs)
    ]
    for load in loads:
        load.start()

    slot_count = pool_ref.shape[2]
    page_len = pool_ref.shape[3]
    dim = pool_ref.shape[4]
    levels = slot_ref.shape[1]
    suffix = q_ref.shape[0]
    heads = q_ref.shape[1] // dim
    per_kv = heads // local_heads
    suffix_pages = suffix // page_len
    factor = math.log2(math.e) / math.sqrt(dim)
    rows = min(ROWS, suffix)
    total = prefix_levels * groups * page_len
    block = max(1, KEY_BLOCK // page_len)

    def wrap(value):
        return lax.rem(value + groups * (levels + 1), groups)

    def falling(k):
        return last - k - jnp.where(last - k <= me, 1, 0)

    def rising(k):
        return k + jnp.where(k >= me, 1, 0)

    low = me < groups // 2
    swap = groups >= 4

    def partner(k, early):
        down = falling(k)
        if early and swap and k < 2:
            down = falling(1 - k)
        return jnp.where(low, down, rising(k))

    for load in loads[:-2]:
        load.wait()
    my_start = start_ref[me]
    my_length = length_ref[me]

    pl.semaphore_wait(barrier, groups - 2 + jnp.where(me == last, 1, 0))

    @pl.when(me == last)
    def _():
        for step in range(1, groups):
            greet(ready, lax.rem(me + step, groups))

    copies = []
    for level in range(prefix_levels):
        for k in range(others):
            place = level * others + k
            target = partner(k, level == 0)
            send[place] = pool_ref[:, :, slot_ref[target, level, me]]
            if level == 0 and k == (1 if swap else 0):

                @pl.when(low & (me != last))
                def _():
                    pl.semaphore_wait(ready, 1)

            if level == 0 and k == others - 1:

                @pl.when(jnp.logical_not(low) & (me != last))
                def _():
                    pl.semaphore_wait(ready, 1)

            copy = pltpu.make_async_remote_copy(
                src_ref=send.at[place],
                dst_ref=recv.at[level * groups + me],
                send_sem=send_sem.at[place],
                recv_sem=recv_sem.at[level * groups + me],
                device_id={"pool": target},
                device_id_type=pl.DeviceIdType.MESH,
            )
            copy.start()
            copies.append(copy)
    loads[-2].wait()
    fresh_copies = []
    for k in range(others):
        target = partner(k, False)
        offset = jnp.minimum(wrap(target - my_start - my_length), suffix_pages - 1)
        fresh_send[k] = own_ref[:, :, offset]
        fresh_copies.append(
            pltpu.make_async_remote_copy(
                src_ref=fresh_send.at[k],
                dst_ref=fresh.at[me],
                send_sem=fresh_send_sem.at[k],
                recv_sem=fresh_recv_sem.at[me],
                device_id={"pool": target},
                device_id_type=pl.DeviceIdType.MESH,
            )
        )

    def arrived(buffer, semaphores, place):
        return pltpu.make_async_remote_copy(
            src_ref=buffer.at[place],
            dst_ref=buffer.at[place],
            send_sem=semaphores.at[place],
            recv_sem=semaphores.at[place],
            device_id={"pool": lax.rem(me + 1, groups)},
            device_id_type=pl.DeviceIdType.MESH,
        )

    fresh[me] = own_ref[:, :, jnp.minimum(wrap(me - my_start - my_length), suffix_pages - 1)]
    for head in range(local_heads):
        own_values[head, :, :dim] = own_ref[1, head].reshape(suffix, dim)
        own_values[head, :, dim:] = jnp.ones((suffix, dim), jnp.bfloat16)
        page_values[head, :, dim:] = jnp.ones((total, dim), jnp.bfloat16)

    far = jnp.where(low, last, 0)
    owners = [me]
    for k in range(groups - 2):
        owner = jnp.where(low, k, k + 1)
        owners.append(owner + jnp.where(owner >= me, 1, 0))
    if groups > 1:
        owners.append(far)
    live = []
    for owner in owners:
        for level in range(prefix_levels):
            live.append(level * groups + wrap(owner - my_start) < my_length)

    def lay(place, page, head):
        span = slice(place * page_len, (place + 1) * page_len)
        page_keys[head, span] = page[0, head]
        page_values[head, span, :dim] = page[1, head]

    for level in range(prefix_levels):
        for head in range(local_heads):
            span = slice(level * page_len, (level + 1) * page_len)
            page_keys[head, span] = pool_ref[0, head, slot_ref[me, level, me]]
            page_values[head, span, :dim] = pool_ref[1, head, slot_ref[me, level, me]]

    masks = {}
    for at in range(0, rows, dim):
        masks[at] = lax.broadcasted_iota(jnp.int32, (rows, dim), 1) + at <= lax.broadcasted_iota(
            jnp.int32, (rows, dim), 0
        )

    def page_pieces(queries, kv_head, first, count):
        scores = lax.dot_general(
            queries,
            page_keys[kv_head, first * page_len : (first + count) * page_len],
            NT,
            preferred_element_type=jnp.float32,
        )
        return [
            jnp.where(live[first + i], scores[:, i * page_len : (i + 1) * page_len], -jnp.inf)
            for i in range(count)
        ]

    def peak_of(pieces):
        return jnp.max(functools.reduce(jnp.maximum, pieces), axis=1, keepdims=True)

    def weigh(pieces, highest):
        return jnp.concatenate(
            [jnp.exp2((piece - highest) * factor).astype(jnp.bfloat16) for piece in pieces], axis=1
        )

    def own_step(head, carry):
        kv_head = head // per_kv
        columns = pl.ds(pl.multiple_of(head * dim, dim), dim)
        for first in range(0, suffix, rows):
            end = first + rows
            queries = q_ref[first:end, columns]
            scores = lax.dot_general(
                queries,
                own_ref[0, kv_head, : end // page_len].reshape(end, dim),
                NT,
                preferred_element_type=jnp.float32,
            )
            pieces = []
            for at in range(0, end, dim):
                piece = scores[:, at : at + dim]
                if at + dim > first + 1:
                    piece = jnp.where(masks[at - first], piece, -jnp.inf)
                pieces.append(piece)
            paged = page_pieces(queries, kv_head, 0, prefix_levels)
            highest = jnp.broadcast_to(peak_of(pieces + paged), (rows, dim))
            acc[head, first:end] = jnp.dot(
                weigh(pieces, highest), own_values[kv_head, :end], preferred_element_type=jnp.float32
            ) + jnp.dot(
                weigh(paged, highest),
                page_values[kv_head, : prefix_levels * page_len],
                preferred_element_type=jnp.float32,
            )
            top[head, first:end] = highest
        return carry

    loads[-1].wait()
    lax.fori_loop(0, heads, own_step, 0, unroll=4)

    for copy in fresh_copies:
        copy.start()

    def page_step(begin, finish, closing, head, carry):
        kv_head = head // per_kv
        columns = pl.ds(pl.multiple_of(head * dim, dim), dim)
        for first in range(0, suffix, rows):
            end = first + rows
            mixed = acc[head, first:end]
            highest = top[head, first:end]
            for place in range(begin, finish, block):
                count = min(block, finish - place)
                pieces = page_pieces(q_ref[first:end, columns], kv_head, place, count)
                risen = jnp.maximum(highest, peak_of(pieces))
                shrink = jnp.exp2((highest - risen) * factor)
                mixed = mixed * jnp.concatenate([shrink, shrink], axis=1) + jnp.dot(
                    weigh(pieces, risen),
                    page_values[kv_head, place * page_len : (place + count) * page_len],
                    preferred_element_type=jnp.float32,
                )
                highest = risen
            if closing:
                out_ref[first:end, columns] = (mixed[:, :dim] / mixed[:, dim:]).astype(jnp.bfloat16)
            else:
                acc[head, first:end] = mixed
                top[head, first:end] = highest
        return carry

    steps = [range(1, groups - 1), range(groups - 1, groups)]
    steps = [step for step in steps if len(step) > 0]
    for number, step in enumerate(steps):
        for i in step:
            for level in range(prefix_levels):
                place = level * groups + owners[i]
                arrived(recv, recv_sem, place).wait_recv()
                for head in range(local_heads):
                    lay(i * prefix_levels + level, recv.at[place], head)
        lax.fori_loop(
            0,
            heads,
            functools.partial(
                page_step,
                step[0] * prefix_levels,
                (step[-1] + 1) * prefix_levels,
                number == len(steps) - 1,
            ),
            0,
            unroll=4,
        )

    places = []
    for request in range(groups):
        length = length_ref[request]
        offset = wrap(me - start_ref[request] - length)
        level = jnp.minimum((length + offset) // groups, levels - 1)
        places.append(jnp.where(offset < suffix_pages, slot_ref[request, level, me], slot_count))

    for copy in copies + fresh_copies:
        copy.wait_send()
    for step in range(1, groups):
        arrived(fresh, fresh_recv_sem, lax.rem(me + step, groups)).wait_recv()
    for slot in range(slot_count):
        chosen = jnp.int32(0)
        hit = jnp.bool_(False)
        for request in range(groups):
            match = places[request] == slot
            chosen = jnp.where(match, request, chosen)
            hit = hit | match
        new_ref[:, :, slot] = jnp.where(hit, fresh[chosen], pool_ref[:, :, slot])


def finish(mixed_ref, pages_ref, out_ref, new_ref, sems):
    page_parts = pages_ref.shape[0] * pages_ref.shape[1]
    count = sems.shape[0] - page_parts
    rows = mixed_ref.shape[0] // count
    copies = []
    for part in range(count):
        span = pl.ds(part * rows, rows)
        copies.append(pltpu.make_async_copy(mixed_ref.at[span], out_ref.at[span], sems.at[part]))
    for part in range(page_parts):
        place = divmod(part, pages_ref.shape[1])
        copies.append(
            pltpu.make_async_copy(pages_ref.at[place], new_ref.at[place], sems.at[count + part])
        )
    for copy in copies:
        copy.start()
    for copy in copies:
        copy.wait()


def body(queries, suffix_kv, pool_kv, prefix_pages, owner_start, page_slot):
    groups = lax.axis_size("pool")
    _, local_heads, slot_count, page_len, dim = pool_kv.shape
    levels = page_slot.shape[2]
    suffix, width = queries.shape
    heads = width // dim
    suffix_pages = suffix // page_len
    prefix_levels = max(1, -(-(groups * levels - suffix_pages) // groups))
    pages = prefix_levels * groups
    page_shape = (2, local_heads, page_len, dim)
    own_shape = (2, local_heads, suffix_pages, page_len, dim)
    vmem = pl.BlockSpec(memory_space=pltpu.VMEM)
    bf16 = jnp.bfloat16
    anywhere = pl.BlockSpec(memory_space=pl.ANY)
    hbm = pl.BlockSpec(memory_space=pltpu.HBM)
    slots = jnp.transpose(page_slot, (0, 2, 1))
    dma = pltpu.SemaphoreType.DMA
    mixed, new_pages = pl.pallas_call(
        functools.partial(exchange, groups, prefix_levels),
        out_shape=(pltpu.VMEM(queries.shape, bf16), pltpu.VMEM(pool_kv.shape, bf16)),
        in_specs=[hbm] * 6,
        out_specs=(vmem, vmem),
        scratch_shapes=[
            pltpu.SMEM(prefix_pages.shape, jnp.int32),
            pltpu.SMEM(owner_start.shape, jnp.int32),
            pltpu.SMEM(slots.shape, jnp.int32),
            pltpu.VMEM(queries.shape, bf16),
            pltpu.VMEM(own_shape, bf16),
            pltpu.VMEM(pool_kv.shape, bf16),
            pltpu.VMEM((prefix_levels * (groups - 1),) + page_shape, bf16),
            pltpu.VMEM((pages,) + page_shape, bf16),
            pltpu.VMEM((groups - 1,) + page_shape, bf16),
            pltpu.VMEM((groups,) + page_shape, bf16),
            pltpu.VMEM((local_heads, suffix, 2 * dim), bf16),
            pltpu.VMEM((local_heads, pages * page_len, dim), bf16),
            pltpu.VMEM((local_heads, pages * page_len, 2 * dim), bf16),
            pltpu.VMEM((heads, suffix, 2 * dim), jnp.float32),
            pltpu.VMEM((heads, suffix, dim), jnp.float32),
            dma((5 + 2 * local_heads,)),
            dma((prefix_levels * (groups - 1),)),
            dma((pages,)),
            dma((groups - 1,)),
            dma((groups,)),
            pltpu.SemaphoreType.REGULAR,
        ],
        compiler_params=pltpu.CompilerParams(
            collective_id=0, has_side_effects=True, vmem_limit_bytes=44 * 1024 * 1024
        ),
    )(
        *(
            pltpu.with_memory_space_constraint(operand, pltpu.HBM)
            for operand in (
                prefix_pages,
                owner_start,
                slots,
                queries,
                suffix_kv.reshape(own_shape),
                pool_kv,
            )
        )
    )
    return pl.pallas_call(
        finish,
        out_shape=(
            jax.ShapeDtypeStruct(queries.shape, bf16),
            jax.ShapeDtypeStruct(pool_kv.shape, bf16),
        ),
        in_specs=[vmem, vmem],
        out_specs=(anywhere, anywhere),
        scratch_shapes=[dma((2 + 2 * local_heads,))],
        compiler_params=pltpu.CompilerParams(vmem_limit_bytes=8 * 1024 * 1024),
    )(mixed, new_pages)


def solution(mesh):
    in_specs = (
        P(("parts", "pool"), "tp"),
        P(None, "tp", ("parts", "pool"), None),
        P(None, "tp", ("parts", "pool"), None, None),
        P("parts"),
        P("parts"),
        P("parts", None, None),
    )
    out_specs = (P(("parts", "pool"), "tp"), P(None, "tp", ("parts", "pool"), None, None))
    return jax.shard_map(body, mesh=mesh, in_specs=in_specs, out_specs=out_specs, check_vma=False)
```

```python
import functools
import math

import jax
import jax.numpy as jnp
from jax import lax
from jax.experimental import pallas as pl
from jax.experimental.pallas import tpu as pltpu
from jax.sharding import PartitionSpec as P

NT = (((1,), (1,)), ((), ()))
ROWS = 256
BATCH = 16
KEY_BLOCK = 512


def exchange(
    groups,
    prefix_levels,
    length_hbm,
    start_hbm,
    slot_hbm,
    q_hbm,
    own_hbm,
    pool_hbm,
    out_ref,
    fresh,
    pool_ref,
    length_ref,
    start_ref,
    slot_ref,
    q_ref,
    own_ref,
    send,
    recv,
    fresh_send,
    own_values,
    page_keys,
    page_values,
    acc,
    top,
    load_sem,
    send_sem,
    recv_sem,
    fresh_send_sem,
    fresh_recv_sem,
    ready,
):
    me = lax.axis_index("pool")
    last = groups - 1
    others = groups - 1

    barrier = pltpu.get_barrier_semaphore()

    def greet(semaphore, device):
        pl.semaphore_signal(
            semaphore, inc=1, device_id={"pool": device}, device_id_type=pl.DeviceIdType.MESH
        )

    @pl.when(me != last)
    def _():
        for step in range(1, groups):
            greet(barrier, lax.rem(me + step, groups))

    local_heads = pool_ref.shape[1]
    pairs = [(length_hbm, length_ref), (start_hbm, start_ref), (slot_hbm, slot_ref)]
    for kind in range(2):
        for head in range(local_heads):
            pairs.append((pool_hbm.at[kind, head], pool_ref.at[kind, head]))
    pairs += [(own_hbm, own_ref), (q_hbm, q_ref)]
    loads = [
        pltpu.make_async_copy(source, target, load_sem.at[i])
        for i, (source, target) in enumerate(pairs)
    ]
    for load in loads:
        load.start()

    slot_count = pool_ref.shape[2]
    page_len = pool_ref.shape[3]
    dim = pool_ref.shape[4]
    levels = slot_ref.shape[1]
    suffix = q_ref.shape[0]
    heads = q_ref.shape[1] // dim
    per_kv = heads // local_heads
    suffix_pages = suffix // page_len
    factor = math.log2(math.e) / math.sqrt(dim)
    rows = min(ROWS, suffix)
    total = prefix_levels * groups * page_len
    batch = math.gcd(heads, BATCH)
    block = max(1, KEY_BLOCK // page_len)

    def wrap(value):
        return lax.rem(value + groups * (levels + 1), groups)

    half = groups // 2
    rest = groups - half
    low = me < half

    def above(k):
        return k + jnp.where(k >= me, 1, 0)

    def below(k):
        return last - k - jnp.where(last - k <= me, 1, 0)

    early = groups >= 4

    def prefix_partner(k):
        down = last - 1 + k if early and k < 2 else below(k)
        up = above(k)
        return jnp.where(low, down, up)

    def suffix_partner(k):
        down = last - k if k < rest - 1 else above(k - rest + 1)
        up = k if k < half - 1 else below(k - half + 1)
        if k == others - 1:
            down, up = half, half - 1
        return jnp.where(low, down, up)

    for load in loads[:-2]:
        load.wait()
    my_start = start_ref[me]
    my_length = length_ref[me]

    pl.semaphore_wait(barrier, groups - 2 + jnp.where(me == last, 1, 0))

    @pl.when(me == last)
    def _():
        for step in range(1, groups):
            greet(ready, lax.rem(me + step, groups))

    copies = []
    for level in range(prefix_levels):
        for k in range(others):
            place = level * others + k
            target = prefix_partner(k)
            send[place] = pool_ref[:, :, slot_ref[target, level, me]]
            if level == 0 and k == (1 if early else 0):

                @pl.when(low & (me != last))
                def _():
                    pl.semaphore_wait(ready, 1)

            if level == 0 and k == others - 1:

                @pl.when(jnp.logical_not(low) & (me != last))
                def _():
                    pl.semaphore_wait(ready, 1)

            copy = pltpu.make_async_remote_copy(
                src_ref=send.at[place],
                dst_ref=recv.at[level * groups + me],
                send_sem=send_sem.at[place],
                recv_sem=recv_sem.at[level * groups + me],
                device_id={"pool": target},
                device_id_type=pl.DeviceIdType.MESH,
            )
            copy.start()
            copies.append(copy)
    loads[-2].wait()
    fresh_copies = []
    for k in range(others):
        target = suffix_partner(k)
        offset = jnp.minimum(wrap(target - my_start - my_length), suffix_pages - 1)
        fresh_send[k] = own_ref[:, :, offset]
        fresh_copies.append(
            pltpu.make_async_remote_copy(
                src_ref=fresh_send.at[k],
                dst_ref=fresh.at[me],
                send_sem=fresh_send_sem.at[k],
                recv_sem=fresh_recv_sem.at[me],
                device_id={"pool": target},
                device_id_type=pl.DeviceIdType.MESH,
            )
        )

    def arrived(buffer, semaphores, place):
        return pltpu.make_async_remote_copy(
            src_ref=buffer.at[place],
            dst_ref=buffer.at[place],
            send_sem=semaphores.at[place],
            recv_sem=semaphores.at[place],
            device_id={"pool": lax.rem(me + 1, groups)},
            device_id_type=pl.DeviceIdType.MESH,
        )

    fresh[me] = own_ref[:, :, jnp.minimum(wrap(me - my_start - my_length), suffix_pages - 1)]
    for copy in fresh_copies:
        copy.start()
    for head in range(local_heads):
        own_values[head, :, :dim] = own_ref[1, head].reshape(suffix, dim)
        own_values[head, :, dim:] = jnp.ones((suffix, dim), jnp.bfloat16)
        page_values[head, :, dim:] = jnp.ones((total, dim), jnp.bfloat16)

    far = jnp.where(low, last, 0)
    owners = []
    for k in range(groups - 2):
        owner = jnp.where(low, k, k + 1)
        owners.append(owner + jnp.where(owner >= me, 1, 0))
    owners.append(me)
    if groups > 1:
        owners.append(far)
    live = []
    for owner in owners:
        for level in range(prefix_levels):
            live.append(level * groups + wrap(owner - my_start) < my_length)

    def lay(place, page, head):
        span = slice(place * page_len, (place + 1) * page_len)
        page_keys[head, span] = page[0, head]
        page_values[head, span, :dim] = page[1, head]

    for level in range(prefix_levels):
        for head in range(local_heads):
            place = max(groups - 2, 0) * prefix_levels + level
            span = slice(place * page_len, (place + 1) * page_len)
            page_keys[head, span] = pool_ref[0, head, slot_ref[me, level, me]]
            page_values[head, span, :dim] = pool_ref[1, head, slot_ref[me, level, me]]

    masks = {}
    for at in range(0, rows, dim):
        masks[at] = lax.broadcasted_iota(jnp.int32, (rows, dim), 1) + at <= lax.broadcasted_iota(
            jnp.int32, (rows, dim), 0
        )

    def page_pieces(queries, kv_head, first, count):
        scores = lax.dot_general(
            queries,
            page_keys[kv_head, first * page_len : (first + count) * page_len],
            NT,
            preferred_element_type=jnp.float32,
        )
        return [
            jnp.where(live[first + i], scores[:, i * page_len : (i + 1) * page_len], -jnp.inf)
            for i in range(count)
        ]

    def peak_of(pieces):
        return jnp.max(functools.reduce(jnp.maximum, pieces), axis=1, keepdims=True)

    def weigh(pieces, highest):
        return jnp.concatenate(
            [jnp.exp2((piece - highest) * factor).astype(jnp.bfloat16) for piece in pieces], axis=1
        )

    def inverse(value):
        guess = pl.reciprocal(value, approx=True)
        return guess * (2.0 - value * guess)

    def in_turn(tasks, scores_of, finish_of):
        scores = scores_of(*tasks[0])
        for i, task in enumerate(tasks):
            following = scores_of(*tasks[i + 1]) if i + 1 < len(tasks) else None
            finish_of(*task, scores)
            scores = following

    def columns_of(head):
        return pl.ds(pl.multiple_of(head * dim, dim), dim)

    def own_scores(head, first):
        end = first + rows
        return lax.dot_general(
            q_ref[first:end, columns_of(head)],
            own_ref[0, head // per_kv, : end // page_len].reshape(end, dim),
            NT,
            preferred_element_type=jnp.float32,
        )

    def own_finish(head, first, scores):
        end = first + rows
        pieces = []
        for at in range(0, end, dim):
            piece = scores[:, at : at + dim]
            if at + dim > first + 1:
                piece = jnp.where(masks[at - first], piece, -jnp.inf)
            pieces.append(piece)
        highest = jnp.broadcast_to(peak_of(pieces), (rows, dim))
        acc[0, head, first:end] = jnp.dot(
            weigh(pieces, highest),
            own_values[head // per_kv, :end],
            preferred_element_type=jnp.float32,
        )
        top[0, head, first:end] = highest

    def own_step(group, carry):
        tasks = [
            (group * batch + i, first) for i in range(batch) for first in range(0, suffix, rows)
        ]
        in_turn(tasks, own_scores, own_finish)
        return carry

    loads[-1].wait()
    lax.fori_loop(0, heads // batch, own_step, 0)


    def page_step(number, place, count, closing, group, carry):
        def scores_of(head, first):
            return page_pieces(q_ref[first : first + rows, columns_of(head)], head // per_kv, place, count)

        def finish_of(head, first, pieces):
            end = first + rows
            highest = top[number % 2, head, first:end]
            risen = jnp.maximum(highest, peak_of(pieces))
            shrink = jnp.exp2((highest - risen) * factor)
            mixed = acc[number % 2, head, first:end] * jnp.concatenate([shrink, shrink], axis=1)
            mixed += jnp.dot(
                weigh(pieces, risen),
                page_values[head // per_kv, place * page_len : (place + count) * page_len],
                preferred_element_type=jnp.float32,
            )
            if closing:
                out_ref[first:end, columns_of(head)] = (
                    mixed[:, :dim] * inverse(mixed[:, dim:])
                ).astype(jnp.bfloat16)
            else:
                acc[(number + 1) % 2, head, first:end] = mixed
                top[(number + 1) % 2, head, first:end] = risen

        tasks = [
            (group * batch + i, first) for i in range(batch) for first in range(0, suffix, rows)
        ]
        in_turn(tasks, scores_of, finish_of)
        return carry

    steps = [range(groups - 2), range(max(groups - 2, 0), groups)]
    steps = [step for step in steps if len(step) > 0]
    calls = 0
    for step in steps:
        for i in step:
            for level in range(prefix_levels):
                if i == groups - 2:
                    continue
                place = level * groups + owners[i]
                arrived(recv, recv_sem, place).wait_recv()
                for head in range(local_heads):
                    lay(i * prefix_levels + level, recv.at[place], head)
        begin, finish = step[0] * prefix_levels, (step[-1] + 1) * prefix_levels
        for place in range(begin, finish, block):
            count = min(block, finish - place)
            closing = place + count == prefix_levels * groups
            lax.fori_loop(
                0,
                heads // batch,
                functools.partial(page_step, calls, place, count, closing),
                0,
            )
            calls += 1

    for copy in copies + fresh_copies:
        copy.wait_send()
    for step in range(1, groups):
        arrived(fresh, fresh_recv_sem, lax.rem(me + step, groups)).wait_recv()


def finish(
    groups,
    length_hbm,
    start_hbm,
    slot_hbm,
    mixed_ref,
    fresh_ref,
    pool_ref,
    out_ref,
    new_ref,
    length_ref,
    start_ref,
    slot_ref,
    load_sem,
    mixed_sem,
    page_sem,
):
    pairs = ((length_hbm, length_ref), (start_hbm, start_ref), (slot_hbm, slot_ref))
    loads = [
        pltpu.make_async_copy(source, target, load_sem.at[i])
        for i, (source, target) in enumerate(pairs)
    ]
    for load in loads:
        load.start()
    store = pltpu.make_async_copy(mixed_ref, out_ref, mixed_sem)
    store.start()
    me = lax.axis_index("pool")
    levels = slot_ref.shape[1]
    slot_count = pool_ref.shape[2]
    suffix_pages = mixed_ref.shape[0] // pool_ref.shape[3]
    for load in loads:
        load.wait()
    targets = []
    for request in range(groups):
        length = length_ref[request]
        offset = lax.rem(me - start_ref[request] - length + groups * (levels + 1), groups)
        level = jnp.minimum((length + offset) // groups, levels - 1)
        target = slot_ref[request, level, me]
        targets.append(jnp.where(offset < suffix_pages, target, slot_count))
    pages = []
    for slot in range(slot_count):
        chosen = jnp.int32(0)
        hit = jnp.bool_(False)
        for request in range(groups):
            match = targets[request] == slot
            chosen = jnp.where(match, request, chosen)
            hit = hit | match
        target = new_ref.at[:, :, slot]
        keep = pltpu.make_async_copy(pool_ref.at[:, :, slot], target, page_sem.at[slot])
        swap = pltpu.make_async_copy(fresh_ref.at[chosen], target, page_sem.at[slot])
        pl.when(jnp.logical_not(hit))(keep.start)
        pl.when(hit)(swap.start)
        pages.append(keep)
    store.wait()
    for page in pages:
        page.wait()


def body(queries, suffix_kv, pool_kv, prefix_pages, owner_start, page_slot):
    groups = lax.axis_size("pool")
    _, local_heads, slot_count, page_len, dim = pool_kv.shape
    levels = page_slot.shape[2]
    suffix, width = queries.shape
    heads = width // dim
    suffix_pages = suffix // page_len
    prefix_levels = max(1, -(-(groups * levels - suffix_pages) // groups))
    pages = prefix_levels * groups
    page_shape = (2, local_heads, page_len, dim)
    own_shape = (2, local_heads, suffix_pages, page_len, dim)
    vmem = pl.BlockSpec(memory_space=pltpu.VMEM)
    bf16 = jnp.bfloat16
    anywhere = pl.BlockSpec(memory_space=pl.ANY)
    hbm = pl.BlockSpec(memory_space=pltpu.HBM)
    slots = jnp.transpose(page_slot, (0, 2, 1))
    dma = pltpu.SemaphoreType.DMA
    scalars = [
        pltpu.SMEM(prefix_pages.shape, jnp.int32),
        pltpu.SMEM(owner_start.shape, jnp.int32),
        pltpu.SMEM(slots.shape, jnp.int32),
    ]
    numbers = [
        pltpu.with_memory_space_constraint(operand, pltpu.HBM)
        for operand in (prefix_pages, owner_start, slots)
    ]
    arrays = [
        pltpu.with_memory_space_constraint(operand, pltpu.HBM)
        for operand in (queries, suffix_kv.reshape(own_shape), pool_kv)
    ]
    mixed, fresh, pool = pl.pallas_call(
        functools.partial(exchange, groups, prefix_levels),
        out_shape=(
            pltpu.VMEM(queries.shape, bf16),
            pltpu.VMEM((groups,) + page_shape, bf16),
            pltpu.VMEM(pool_kv.shape, bf16),
        ),
        in_specs=[hbm] * 6,
        out_specs=(vmem, vmem, vmem),
        scratch_shapes=scalars
        + [
            pltpu.VMEM(queries.shape, bf16),
            pltpu.VMEM(own_shape, bf16),
            pltpu.VMEM((prefix_levels * (groups - 1),) + page_shape, bf16),
            pltpu.VMEM((pages,) + page_shape, bf16),
            pltpu.VMEM((groups - 1,) + page_shape, bf16),
            pltpu.VMEM((local_heads, suffix, 2 * dim), bf16),
            pltpu.VMEM((local_heads, pages * page_len, dim), bf16),
            pltpu.VMEM((local_heads, pages * page_len, 2 * dim), bf16),
            pltpu.VMEM((2, heads, suffix, 2 * dim), jnp.float32),
            pltpu.VMEM((2, heads, suffix, dim), jnp.float32),
            dma((5 + 2 * local_heads,)),
            dma((prefix_levels * (groups - 1),)),
            dma((pages,)),
            dma((groups - 1,)),
            dma((groups,)),
            pltpu.SemaphoreType.REGULAR,
        ],
        compiler_params=pltpu.CompilerParams(
            collective_id=0, has_side_effects=True, vmem_limit_bytes=44 * 1024 * 1024
        ),
    )(*numbers, *arrays)
    return pl.pallas_call(
        functools.partial(finish, groups),
        out_shape=(
            jax.ShapeDtypeStruct(queries.shape, bf16),
            jax.ShapeDtypeStruct(pool_kv.shape, bf16),
        ),
        in_specs=[hbm, hbm, hbm, vmem, vmem, vmem],
        out_specs=(anywhere, anywhere),
        scratch_shapes=scalars + [dma((3,)), dma, dma((slot_count,))],
        compiler_params=pltpu.CompilerParams(vmem_limit_bytes=8 * 1024 * 1024),
    )(*numbers, mixed, fresh, pool)


def solution(mesh):
    in_specs = (
        P(("parts", "pool"), "tp"),
        P(None, "tp", ("parts", "pool"), None),
        P(None, "tp", ("parts", "pool"), None, None),
        P("parts"),
        P("parts"),
        P("parts", None, None),
    )
    out_specs = (P(("parts", "pool"), "tp"), P(None, "tp", ("parts", "pool"), None, None))
    return jax.shard_map(body, mesh=mesh, in_specs=in_specs, out_specs=out_specs, check_vma=False)
```

```python
import functools
import math

import jax
import jax.numpy as jnp
from jax import lax
from jax.experimental import pallas as pl
from jax.experimental.pallas import tpu as pltpu
from jax.sharding import PartitionSpec as P

NT = (((1,), (1,)), ((), ()))
ROWS = 256
BATCH = 16
KEY_BLOCK = 512


def exchange(
    groups,
    prefix_levels,
    length_hbm,
    start_hbm,
    slot_hbm,
    q_hbm,
    own_hbm,
    pool_hbm,
    out_ref,
    fresh,
    pool_ref,
    length_ref,
    start_ref,
    slot_ref,
    q_ref,
    own_ref,
    send,
    recv,
    fresh_send,
    own_values,
    page_keys,
    page_values,
    acc,
    top,
    load_sem,
    send_sem,
    recv_sem,
    fresh_send_sem,
    fresh_recv_sem,
    ready,
):
    me = lax.axis_index("pool")
    last = groups - 1
    others = groups - 1

    barrier = pltpu.get_barrier_semaphore()

    def greet(semaphore, device):
        pl.semaphore_signal(
            semaphore, inc=1, device_id={"pool": device}, device_id_type=pl.DeviceIdType.MESH
        )

    @pl.when(me != last)
    def _():
        for step in range(1, groups):
            greet(barrier, lax.rem(me + step, groups))

    local_heads = pool_ref.shape[1]
    pairs = [(length_hbm, length_ref), (start_hbm, start_ref), (slot_hbm, slot_ref)]
    for kind in range(2):
        for head in range(local_heads):
            pairs.append((pool_hbm.at[kind, head], pool_ref.at[kind, head]))
    pairs += [(own_hbm, own_ref), (q_hbm, q_ref)]
    loads = [
        pltpu.make_async_copy(source, target, load_sem.at[i])
        for i, (source, target) in enumerate(pairs)
    ]
    for load in loads:
        load.start()

    slot_count = pool_ref.shape[2]
    page_len = pool_ref.shape[3]
    dim = pool_ref.shape[4]
    levels = slot_ref.shape[1]
    suffix = q_ref.shape[0]
    heads = q_ref.shape[1] // dim
    per_kv = heads // local_heads
    suffix_pages = suffix // page_len
    factor = math.log2(math.e) / math.sqrt(dim)
    rows = min(ROWS, suffix)
    total = prefix_levels * groups * page_len
    batch = math.gcd(heads, BATCH)
    block = max(1, KEY_BLOCK // page_len)

    def wrap(value):
        return lax.rem(value + groups * (levels + 1), groups)

    half = groups // 2
    rest = groups - half
    low = me < half

    def above(k):
        return k + jnp.where(k >= me, 1, 0)

    def below(k):
        return last - k - jnp.where(last - k <= me, 1, 0)

    early = groups >= 4

    def prefix_partner(k):
        down = last - 1 + k if early and k < 2 else below(k)
        up = above(k)
        return jnp.where(low, down, up)

    def suffix_partner(k):
        down = last - k if k < rest - 1 else above(k - rest + 1)
        up = k if k < half - 1 else below(k - half + 1)
        if k == others - 1:
            down, up = half, half - 1
        return jnp.where(low, down, up)

    pl.semaphore_wait(barrier, groups - 2 + jnp.where(me == last, 1, 0))

    @pl.when(me == last)
    def _():
        for step in range(1, groups):
            greet(ready, lax.rem(me + step, groups))

    for load in loads[:-2]:
        load.wait()
    my_start = start_ref[me]
    my_length = length_ref[me]

    copies = []
    for level in range(prefix_levels):
        for k in range(others):
            place = level * others + k
            target = prefix_partner(k)
            send[place] = pool_ref[:, :, slot_ref[target, level, me]]
            if level == 0 and k == (1 if early else 0):

                @pl.when(low & (me != last))
                def _():
                    pl.semaphore_wait(ready, 1)

            if level == 0 and k == others - 1:

                @pl.when(jnp.logical_not(low) & (me != last))
                def _():
                    pl.semaphore_wait(ready, 1)

            copy = pltpu.make_async_remote_copy(
                src_ref=send.at[place],
                dst_ref=recv.at[level * groups + me],
                send_sem=send_sem.at[place],
                recv_sem=recv_sem.at[level * groups + me],
                device_id={"pool": target},
                device_id_type=pl.DeviceIdType.MESH,
            )
            copy.start()
            copies.append(copy)
    loads[-2].wait()
    fresh_copies = []
    for k in range(others):
        target = suffix_partner(k)
        offset = jnp.minimum(wrap(target - my_start - my_length), suffix_pages - 1)
        fresh_send[k] = own_ref[:, :, offset]
        fresh_copies.append(
            pltpu.make_async_remote_copy(
                src_ref=fresh_send.at[k],
                dst_ref=fresh.at[me],
                send_sem=fresh_send_sem.at[k],
                recv_sem=fresh_recv_sem.at[me],
                device_id={"pool": target},
                device_id_type=pl.DeviceIdType.MESH,
            )
        )

    def arrived(buffer, semaphores, place):
        return pltpu.make_async_remote_copy(
            src_ref=buffer.at[place],
            dst_ref=buffer.at[place],
            send_sem=semaphores.at[place],
            recv_sem=semaphores.at[place],
            device_id={"pool": lax.rem(me + 1, groups)},
            device_id_type=pl.DeviceIdType.MESH,
        )

    fresh[me] = own_ref[:, :, jnp.minimum(wrap(me - my_start - my_length), suffix_pages - 1)]
    second = lax.rem(lax.axis_index("tp"), 2) == 1
    for copy in fresh_copies[:-1]:
        copy.start()
    for copy in fresh_copies[-1:]:
        pl.when(jnp.logical_not(second))(copy.start)
    for head in range(local_heads):
        own_values[head, :, :dim] = own_ref[1, head].reshape(suffix, dim)
        own_values[head, :, dim:] = jnp.ones((suffix, dim), jnp.bfloat16)
        page_values[head, :, dim:] = jnp.ones((total, dim), jnp.bfloat16)

    far = jnp.where(low, last, 0)
    owners = []
    for k in range(groups - 2):
        owner = jnp.where(low, k, k + 1)
        owners.append(owner + jnp.where(owner >= me, 1, 0))
    owners.append(me)
    if groups > 1:
        owners.append(far)
    live = []
    for owner in owners:
        for level in range(prefix_levels):
            live.append(level * groups + wrap(owner - my_start) < my_length)

    def lay(place, page, head):
        span = slice(place * page_len, (place + 1) * page_len)
        page_keys[head, span] = page[0, head]
        page_values[head, span, :dim] = page[1, head]

    for level in range(prefix_levels):
        for head in range(local_heads):
            place = max(groups - 2, 0) * prefix_levels + level
            span = slice(place * page_len, (place + 1) * page_len)
            page_keys[head, span] = pool_ref[0, head, slot_ref[me, level, me]]
            page_values[head, span, :dim] = pool_ref[1, head, slot_ref[me, level, me]]

    masks = {}
    for at in range(0, rows, dim):
        masks[at] = lax.broadcasted_iota(jnp.int32, (rows, dim), 1) + at <= lax.broadcasted_iota(
            jnp.int32, (rows, dim), 0
        )

    def page_pieces(queries, kv_head, first, count):
        scores = lax.dot_general(
            queries,
            page_keys[kv_head, first * page_len : (first + count) * page_len],
            NT,
            preferred_element_type=jnp.float32,
        )
        return [
            jnp.where(live[first + i], scores[:, i * page_len : (i + 1) * page_len], -jnp.inf)
            for i in range(count)
        ]

    def peak_of(pieces):
        return jnp.max(functools.reduce(jnp.maximum, pieces), axis=1, keepdims=True)

    def weigh(pieces, highest):
        return jnp.concatenate(
            [jnp.exp2((piece - highest) * factor).astype(jnp.bfloat16) for piece in pieces], axis=1
        )

    def inverse(value):
        guess = pl.reciprocal(value, approx=True)
        return guess * (2.0 - value * guess)

    def in_turn(tasks, scores_of, finish_of):
        scores = scores_of(*tasks[0])
        for i, task in enumerate(tasks):
            following = scores_of(*tasks[i + 1]) if i + 1 < len(tasks) else None
            finish_of(*task, scores)
            scores = following

    def columns_of(head):
        return pl.ds(pl.multiple_of(head * dim, dim), dim)

    def own_scores(head, first):
        end = first + rows
        return lax.dot_general(
            q_ref[first:end, columns_of(head)],
            own_ref[0, head // per_kv, : end // page_len].reshape(end, dim),
            NT,
            preferred_element_type=jnp.float32,
        )

    def own_finish(head, first, scores):
        end = first + rows
        pieces = []
        for at in range(0, end, dim):
            piece = scores[:, at : at + dim]
            if at + dim > first + 1:
                piece = jnp.where(masks[at - first], piece, -jnp.inf)
            pieces.append(piece)
        highest = jnp.broadcast_to(peak_of(pieces), (rows, dim))
        acc[0, head, first:end] = jnp.dot(
            weigh(pieces, highest),
            own_values[head // per_kv, :end],
            preferred_element_type=jnp.float32,
        )
        top[0, head, first:end] = highest

    def own_step(group, carry):
        tasks = [
            (group * batch + i, first) for i in range(batch) for first in range(0, suffix, rows)
        ]
        in_turn(tasks, own_scores, own_finish)
        return carry

    loads[-1].wait()
    lax.fori_loop(0, heads // batch, own_step, 0)
    for copy in fresh_copies[-1:]:
        pl.when(second)(copy.start)


    def page_step(number, place, count, closing, group, carry):
        def scores_of(head, first):
            return page_pieces(q_ref[first : first + rows, columns_of(head)], head // per_kv, place, count)

        def finish_of(head, first, pieces):
            end = first + rows
            highest = top[number % 2, head, first:end]
            risen = jnp.maximum(highest, peak_of(pieces))
            shrink = jnp.exp2((highest - risen) * factor)
            mixed = acc[number % 2, head, first:end] * jnp.concatenate([shrink, shrink], axis=1)
            mixed += jnp.dot(
                weigh(pieces, risen),
                page_values[head // per_kv, place * page_len : (place + count) * page_len],
                preferred_element_type=jnp.float32,
            )
            if closing:
                out_ref[first:end, columns_of(head)] = (
                    mixed[:, :dim] * inverse(mixed[:, dim:])
                ).astype(jnp.bfloat16)
            else:
                acc[(number + 1) % 2, head, first:end] = mixed
                top[(number + 1) % 2, head, first:end] = risen

        tasks = [
            (group * batch + i, first) for i in range(batch) for first in range(0, suffix, rows)
        ]
        in_turn(tasks, scores_of, finish_of)
        return carry

    steps = [range(groups - 2), range(max(groups - 2, 0), groups)]
    steps = [step for step in steps if len(step) > 0]
    calls = 0
    for step in steps:
        for i in step:
            for level in range(prefix_levels):
                if i == groups - 2:
                    continue
                place = level * groups + owners[i]
                arrived(recv, recv_sem, place).wait_recv()
                for head in range(local_heads):
                    lay(i * prefix_levels + level, recv.at[place], head)
        begin, finish = step[0] * prefix_levels, (step[-1] + 1) * prefix_levels
        for place in range(begin, finish, block):
            count = min(block, finish - place)
            closing = place + count == prefix_levels * groups
            lax.fori_loop(
                0,
                heads // batch,
                functools.partial(page_step, calls, place, count, closing),
                0,
            )
            calls += 1

    for copy in copies + fresh_copies:
        copy.wait_send()
    for step in range(1, groups):
        arrived(fresh, fresh_recv_sem, lax.rem(me + step, groups)).wait_recv()


def finish(
    groups,
    length_hbm,
    start_hbm,
    slot_hbm,
    mixed_ref,
    fresh_ref,
    pool_ref,
    out_ref,
    new_ref,
    length_ref,
    start_ref,
    slot_ref,
    load_sem,
    mixed_sem,
    page_sem,
):
    pairs = ((length_hbm, length_ref), (start_hbm, start_ref), (slot_hbm, slot_ref))
    loads = [
        pltpu.make_async_copy(source, target, load_sem.at[i])
        for i, (source, target) in enumerate(pairs)
    ]
    for load in loads:
        load.start()
    store = pltpu.make_async_copy(mixed_ref, out_ref, mixed_sem)
    store.start()
    me = lax.axis_index("pool")
    levels = slot_ref.shape[1]
    slot_count = pool_ref.shape[2]
    suffix_pages = mixed_ref.shape[0] // pool_ref.shape[3]
    for load in loads:
        load.wait()
    targets = []
    for request in range(groups):
        length = length_ref[request]
        offset = lax.rem(me - start_ref[request] - length + groups * (levels + 1), groups)
        level = jnp.minimum((length + offset) // groups, levels - 1)
        target = slot_ref[request, level, me]
        targets.append(jnp.where(offset < suffix_pages, target, slot_count))
    pages = []
    for slot in range(slot_count):
        chosen = jnp.int32(0)
        hit = jnp.bool_(False)
        for request in range(groups):
            match = targets[request] == slot
            chosen = jnp.where(match, request, chosen)
            hit = hit | match
        target = new_ref.at[:, :, slot]
        keep = pltpu.make_async_copy(pool_ref.at[:, :, slot], target, page_sem.at[slot])
        swap = pltpu.make_async_copy(fresh_ref.at[chosen], target, page_sem.at[slot])
        pl.when(jnp.logical_not(hit))(keep.start)
        pl.when(hit)(swap.start)
        pages.append(keep)
    store.wait()
    for page in pages:
        page.wait()


def body(queries, suffix_kv, pool_kv, prefix_pages, owner_start, page_slot):
    groups = lax.axis_size("pool")
    _, local_heads, slot_count, page_len, dim = pool_kv.shape
    levels = page_slot.shape[2]
    suffix, width = queries.shape
    heads = width // dim
    suffix_pages = suffix // page_len
    prefix_levels = max(1, -(-(groups * levels - suffix_pages) // groups))
    pages = prefix_levels * groups
    page_shape = (2, local_heads, page_len, dim)
    own_shape = (2, local_heads, suffix_pages, page_len, dim)
    vmem = pl.BlockSpec(memory_space=pltpu.VMEM)
    bf16 = jnp.bfloat16
    anywhere = pl.BlockSpec(memory_space=pl.ANY)
    hbm = pl.BlockSpec(memory_space=pltpu.HBM)
    slots = jnp.transpose(page_slot, (0, 2, 1))
    dma = pltpu.SemaphoreType.DMA
    scalars = [
        pltpu.SMEM(prefix_pages.shape, jnp.int32),
        pltpu.SMEM(owner_start.shape, jnp.int32),
        pltpu.SMEM(slots.shape, jnp.int32),
    ]
    numbers = [
        pltpu.with_memory_space_constraint(operand, pltpu.HBM)
        for operand in (prefix_pages, owner_start, slots)
    ]
    arrays = [
        pltpu.with_memory_space_constraint(operand, pltpu.HBM)
        for operand in (queries, suffix_kv.reshape(own_shape), pool_kv)
    ]
    mixed, fresh, pool = pl.pallas_call(
        functools.partial(exchange, groups, prefix_levels),
        out_shape=(
            pltpu.VMEM(queries.shape, bf16),
            pltpu.VMEM((groups,) + page_shape, bf16),
            pltpu.VMEM(pool_kv.shape, bf16),
        ),
        in_specs=[hbm] * 6,
        out_specs=(vmem, vmem, vmem),
        scratch_shapes=scalars
        + [
            pltpu.VMEM(queries.shape, bf16),
            pltpu.VMEM(own_shape, bf16),
            pltpu.VMEM((prefix_levels * (groups - 1),) + page_shape, bf16),
            pltpu.VMEM((pages,) + page_shape, bf16),
            pltpu.VMEM((groups - 1,) + page_shape, bf16),
            pltpu.VMEM((local_heads, suffix, 2 * dim), bf16),
            pltpu.VMEM((local_heads, pages * page_len, dim), bf16),
            pltpu.VMEM((local_heads, pages * page_len, 2 * dim), bf16),
            pltpu.VMEM((2, heads, suffix, 2 * dim), jnp.float32),
            pltpu.VMEM((2, heads, suffix, dim), jnp.float32),
            dma((5 + 2 * local_heads,)),
            dma((prefix_levels * (groups - 1),)),
            dma((pages,)),
            dma((groups - 1,)),
            dma((groups,)),
            pltpu.SemaphoreType.REGULAR,
        ],
        compiler_params=pltpu.CompilerParams(
            collective_id=0, has_side_effects=True, vmem_limit_bytes=44 * 1024 * 1024
        ),
    )(*numbers, *arrays)
    return pl.pallas_call(
        functools.partial(finish, groups),
        out_shape=(
            jax.ShapeDtypeStruct(queries.shape, bf16),
            jax.ShapeDtypeStruct(pool_kv.shape, bf16),
        ),
        in_specs=[hbm, hbm, hbm, vmem, vmem, vmem],
        out_specs=(anywhere, anywhere),
        scratch_shapes=scalars + [dma((3,)), dma, dma((slot_count,))],
        compiler_params=pltpu.CompilerParams(vmem_limit_bytes=8 * 1024 * 1024),
    )(*numbers, mixed, fresh, pool)


def solution(mesh):
    in_specs = (
        P(("parts", "pool"), "tp"),
        P(None, "tp", ("parts", "pool"), None),
        P(None, "tp", ("parts", "pool"), None, None),
        P("parts"),
        P("parts"),
        P("parts", None, None),
    )
    out_specs = (P(("parts", "pool"), "tp"), P(None, "tp", ("parts", "pool"), None, None))
    return jax.shard_map(body, mesh=mesh, in_specs=in_specs, out_specs=out_specs, check_vma=False)
```

```python
import functools
import math

import jax
import jax.numpy as jnp
from jax import lax
from jax.experimental import pallas as pl
from jax.experimental.pallas import tpu as pltpu
from jax.sharding import PartitionSpec as P

NT = (((1,), (1,)), ((), ()))
ROWS = 256
BATCH = 16
KEY_BLOCK = 512


def exchange(
    groups,
    prefix_levels,
    length_hbm,
    start_hbm,
    slot_hbm,
    q_hbm,
    own_hbm,
    pool_hbm,
    out_ref,
    fresh,
    pool_ref,
    length_ref,
    start_ref,
    slot_ref,
    q_ref,
    own_ref,
    first_keys,
    send,
    recv,
    fresh_send,
    own_values,
    page_keys,
    page_values,
    acc,
    top,
    load_sem,
    send_sem,
    recv_sem,
    fresh_send_sem,
    fresh_recv_sem,
    ready,
):
    me = lax.axis_index("pool")
    last = groups - 1
    others = groups - 1

    barrier = pltpu.get_barrier_semaphore()

    def greet(semaphore, device):
        pl.semaphore_signal(
            semaphore, inc=1, device_id={"pool": device}, device_id_type=pl.DeviceIdType.MESH
        )

    local_heads = pool_ref.shape[1]
    pairs = [(length_hbm, length_ref), (start_hbm, start_ref), (slot_hbm, slot_ref)]
    pairs.append((pool_hbm.at[0], first_keys))
    for kind in range(2):
        for head in range(local_heads):
            pairs.append((pool_hbm.at[kind, head], pool_ref.at[kind, head]))
    pairs += [(own_hbm, own_ref), (q_hbm, q_ref)]
    loads = [
        pltpu.make_async_copy(source, target, load_sem.at[i])
        for i, (source, target) in enumerate(pairs)
    ]
    for load in loads:
        load.start()

    @pl.when(me != last)
    def _():
        for step in range(1, groups):
            greet(barrier, lax.rem(me + step, groups))

    slot_count = pool_ref.shape[2]
    page_len = pool_ref.shape[3]
    dim = pool_ref.shape[4]
    levels = slot_ref.shape[1]
    suffix = q_ref.shape[0]
    heads = q_ref.shape[1] // dim
    per_kv = heads // local_heads
    suffix_pages = suffix // page_len
    factor = math.log2(math.e) / math.sqrt(dim)
    rows = min(ROWS, suffix)
    total = prefix_levels * groups * page_len
    batch = math.gcd(heads, BATCH)
    block = max(1, KEY_BLOCK // page_len)

    def wrap(value):
        return lax.rem(value + groups * (levels + 1), groups)

    half = groups // 2
    rest = groups - half
    low = me < half

    def above(k):
        return k + jnp.where(k >= me, 1, 0)

    def below(k):
        return last - k - jnp.where(last - k <= me, 1, 0)

    early = groups >= 4

    def prefix_partner(k):
        down = last - 1 + k if early and k < 2 else below(k)
        up = above(k)
        return jnp.where(low, down, up)

    def suffix_partner(k):
        down = last - k if k < rest - 1 else above(k - rest + 1)
        up = k if k < half - 1 else below(k - half + 1)
        if k == others - 1:
            down, up = half, half - 1
        return jnp.where(low, down, up)

    pl.semaphore_wait(barrier, groups - 2 + jnp.where(me == last, 1, 0))

    @pl.when(me == last)
    def _():
        for step in range(1, groups):
            greet(ready, lax.rem(me + step, groups))

    for load in loads[:4]:
        load.wait()
    my_start = start_ref[me]
    my_length = length_ref[me]

    copies = []
    for level in range(prefix_levels):
        for k in range(others):
            place = level * others + k
            target = prefix_partner(k)
            opening = level == 0 and k == 0
            if not opening:
                send[place] = pool_ref[:, :, slot_ref[target, level, me]]
            if level == 0 and k == (1 if early else 0):

                @pl.when(low & (me != last))
                def _():
                    pl.semaphore_wait(ready, 1)

            if level == 0 and k == others - 1:

                @pl.when(jnp.logical_not(low) & (me != last))
                def _():
                    pl.semaphore_wait(ready, 1)

            copy = pltpu.make_async_remote_copy(
                src_ref=send.at[place],
                dst_ref=recv.at[level * groups + me],
                send_sem=send_sem.at[place],
                recv_sem=recv_sem.at[level * groups + me],
                device_id={"pool": target},
                device_id_type=pl.DeviceIdType.MESH,
            )
            if opening:
                for kind in range(2):
                    if kind == 0:
                        send[place, kind] = first_keys[:, slot_ref[target, level, me]]
                    else:
                        for load in loads[4:-2]:
                            load.wait()
                        send[place, kind] = pool_ref[kind, :, slot_ref[target, level, me]]
                    pltpu.make_async_remote_copy(
                        src_ref=send.at[place, kind],
                        dst_ref=recv.at[level * groups + me, kind],
                        send_sem=send_sem.at[place],
                        recv_sem=recv_sem.at[level * groups + me],
                        device_id={"pool": target},
                        device_id_type=pl.DeviceIdType.MESH,
                    ).start()
            else:
                copy.start()
            copies.append(copy)
    loads[-2].wait()
    fresh_copies = []
    for k in range(others):
        target = suffix_partner(k)
        offset = jnp.minimum(wrap(target - my_start - my_length), suffix_pages - 1)
        fresh_send[k] = own_ref[:, :, offset]
        fresh_copies.append(
            pltpu.make_async_remote_copy(
                src_ref=fresh_send.at[k],
                dst_ref=fresh.at[me],
                send_sem=fresh_send_sem.at[k],
                recv_sem=fresh_recv_sem.at[me],
                device_id={"pool": target},
                device_id_type=pl.DeviceIdType.MESH,
            )
        )

    def arrived(buffer, semaphores, place):
        return pltpu.make_async_remote_copy(
            src_ref=buffer.at[place],
            dst_ref=buffer.at[place],
            send_sem=semaphores.at[place],
            recv_sem=semaphores.at[place],
            device_id={"pool": lax.rem(me + 1, groups)},
            device_id_type=pl.DeviceIdType.MESH,
        )

    fresh[me] = own_ref[:, :, jnp.minimum(wrap(me - my_start - my_length), suffix_pages - 1)]
    second = lax.rem(lax.axis_index("tp"), 2) == 1
    for copy in fresh_copies[:-1]:
        copy.start()
    for copy in fresh_copies[-1:]:
        pl.when(jnp.logical_not(second))(copy.start)
    for head in range(local_heads):
        own_values[head, :, :dim] = own_ref[1, head].reshape(suffix, dim)
        own_values[head, :, dim:] = jnp.ones((suffix, dim), jnp.bfloat16)
        page_values[head, :, dim:] = jnp.ones((total, dim), jnp.bfloat16)

    far = jnp.where(low, last, 0)
    owners = []
    for k in range(groups - 2):
        owner = jnp.where(low, k, k + 1)
        owners.append(owner + jnp.where(owner >= me, 1, 0))
    owners.append(me)
    if groups > 1:
        owners.append(far)
    live = []
    for owner in owners:
        for level in range(prefix_levels):
            live.append(level * groups + wrap(owner - my_start) < my_length)

    def lay(place, page, head):
        span = slice(place * page_len, (place + 1) * page_len)
        page_keys[head, span] = page[0, head]
        page_values[head, span, :dim] = page[1, head]

    for level in range(prefix_levels):
        for head in range(local_heads):
            place = max(groups - 2, 0) * prefix_levels + level
            span = slice(place * page_len, (place + 1) * page_len)
            page_keys[head, span] = pool_ref[0, head, slot_ref[me, level, me]]
            page_values[head, span, :dim] = pool_ref[1, head, slot_ref[me, level, me]]

    masks = {}
    for at in range(0, rows, dim):
        masks[at] = lax.broadcasted_iota(jnp.int32, (rows, dim), 1) + at <= lax.broadcasted_iota(
            jnp.int32, (rows, dim), 0
        )

    def page_pieces(queries, kv_head, first, count):
        scores = lax.dot_general(
            queries,
            page_keys[kv_head, first * page_len : (first + count) * page_len],
            NT,
            preferred_element_type=jnp.float32,
        )
        return [
            jnp.where(live[first + i], scores[:, i * page_len : (i + 1) * page_len], -jnp.inf)
            for i in range(count)
        ]

    def peak_of(pieces):
        return jnp.max(functools.reduce(jnp.maximum, pieces), axis=1, keepdims=True)

    def weigh(pieces, highest):
        return jnp.concatenate(
            [jnp.exp2((piece - highest) * factor).astype(jnp.bfloat16) for piece in pieces], axis=1
        )

    def inverse(value):
        guess = pl.reciprocal(value, approx=True)
        return guess * (2.0 - value * guess)

    def in_turn(tasks, scores_of, finish_of):
        scores = scores_of(*tasks[0])
        for i, task in enumerate(tasks):
            following = scores_of(*tasks[i + 1]) if i + 1 < len(tasks) else None
            finish_of(*task, scores)
            scores = following

    def columns_of(head):
        return pl.ds(pl.multiple_of(head * dim, dim), dim)

    def own_scores(head, first):
        end = first + rows
        return lax.dot_general(
            q_ref[first:end, columns_of(head)],
            own_ref[0, head // per_kv, : end // page_len].reshape(end, dim),
            NT,
            preferred_element_type=jnp.float32,
        )

    def own_finish(head, first, scores):
        end = first + rows
        pieces = []
        for at in range(0, end, dim):
            piece = scores[:, at : at + dim]
            if at + dim > first + 1:
                piece = jnp.where(masks[at - first], piece, -jnp.inf)
            pieces.append(piece)
        highest = jnp.broadcast_to(peak_of(pieces), (rows, dim))
        acc[0, head, first:end] = jnp.dot(
            weigh(pieces, highest),
            own_values[head // per_kv, :end],
            preferred_element_type=jnp.float32,
        )
        top[0, head, first:end] = highest

    def own_step(group, carry):
        tasks = [
            (group * batch + i, first) for i in range(batch) for first in range(0, suffix, rows)
        ]
        in_turn(tasks, own_scores, own_finish)
        return carry

    loads[-1].wait()
    lax.fori_loop(0, heads // batch, own_step, 0)
    for copy in fresh_copies[-1:]:
        pl.when(second)(copy.start)


    def page_step(number, place, count, closing, group, carry):
        def scores_of(head, first):
            return page_pieces(q_ref[first : first + rows, columns_of(head)], head // per_kv, place, count)

        def finish_of(head, first, pieces):
            end = first + rows
            highest = top[number % 2, head, first:end]
            risen = jnp.maximum(highest, peak_of(pieces))
            shrink = jnp.exp2((highest - risen) * factor)
            mixed = acc[number % 2, head, first:end] * jnp.concatenate([shrink, shrink], axis=1)
            mixed += jnp.dot(
                weigh(pieces, risen),
                page_values[head // per_kv, place * page_len : (place + count) * page_len],
                preferred_element_type=jnp.float32,
            )
            if closing:
                out_ref[first:end, columns_of(head)] = (
                    mixed[:, :dim] * inverse(mixed[:, dim:])
                ).astype(jnp.bfloat16)
            else:
                acc[(number + 1) % 2, head, first:end] = mixed
                top[(number + 1) % 2, head, first:end] = risen

        tasks = [
            (group * batch + i, first) for i in range(batch) for first in range(0, suffix, rows)
        ]
        in_turn(tasks, scores_of, finish_of)
        return carry

    steps = [range(groups - 2), range(max(groups - 2, 0), groups)]
    steps = [step for step in steps if len(step) > 0]
    calls = 0
    for step in steps:
        for i in step:
            for level in range(prefix_levels):
                if i == groups - 2:
                    continue
                place = level * groups + owners[i]
                arrived(recv, recv_sem, place).wait_recv()
                for head in range(local_heads):
                    lay(i * prefix_levels + level, recv.at[place], head)
        begin, finish = step[0] * prefix_levels, (step[-1] + 1) * prefix_levels
        for place in range(begin, finish, block):
            count = min(block, finish - place)
            closing = place + count == prefix_levels * groups
            lax.fori_loop(
                0,
                heads // batch,
                functools.partial(page_step, calls, place, count, closing),
                0,
            )
            calls += 1

    for copy in copies + fresh_copies:
        copy.wait_send()
    for step in range(1, groups):
        arrived(fresh, fresh_recv_sem, lax.rem(me + step, groups)).wait_recv()


def finish(
    groups,
    length_hbm,
    start_hbm,
    slot_hbm,
    mixed_ref,
    fresh_ref,
    pool_ref,
    out_ref,
    new_ref,
    length_ref,
    start_ref,
    slot_ref,
    load_sem,
    mixed_sem,
    page_sem,
):
    pairs = ((length_hbm, length_ref), (start_hbm, start_ref), (slot_hbm, slot_ref))
    loads = [
        pltpu.make_async_copy(source, target, load_sem.at[i])
        for i, (source, target) in enumerate(pairs)
    ]
    for load in loads:
        load.start()
    store = pltpu.make_async_copy(mixed_ref, out_ref, mixed_sem)
    store.start()
    me = lax.axis_index("pool")
    levels = slot_ref.shape[1]
    slot_count = pool_ref.shape[2]
    suffix_pages = mixed_ref.shape[0] // pool_ref.shape[3]
    for load in loads:
        load.wait()
    targets = []
    for request in range(groups):
        length = length_ref[request]
        offset = lax.rem(me - start_ref[request] - length + groups * (levels + 1), groups)
        level = jnp.minimum((length + offset) // groups, levels - 1)
        target = slot_ref[request, level, me]
        targets.append(jnp.where(offset < suffix_pages, target, slot_count))
    pages = []
    for slot in range(slot_count):
        chosen = jnp.int32(0)
        hit = jnp.bool_(False)
        for request in range(groups):
            match = targets[request] == slot
            chosen = jnp.where(match, request, chosen)
            hit = hit | match
        target = new_ref.at[:, :, slot]
        keep = pltpu.make_async_copy(pool_ref.at[:, :, slot], target, page_sem.at[slot])
        swap = pltpu.make_async_copy(fresh_ref.at[chosen], target, page_sem.at[slot])
        pl.when(jnp.logical_not(hit))(keep.start)
        pl.when(hit)(swap.start)
        pages.append(keep)
    store.wait()
    for page in pages:
        page.wait()


def body(queries, suffix_kv, pool_kv, prefix_pages, owner_start, page_slot):
    groups = lax.axis_size("pool")
    _, local_heads, slot_count, page_len, dim = pool_kv.shape
    levels = page_slot.shape[2]
    suffix, width = queries.shape
    heads = width // dim
    suffix_pages = suffix // page_len
    prefix_levels = max(1, -(-(groups * levels - suffix_pages) // groups))
    pages = prefix_levels * groups
    page_shape = (2, local_heads, page_len, dim)
    own_shape = (2, local_heads, suffix_pages, page_len, dim)
    vmem = pl.BlockSpec(memory_space=pltpu.VMEM)
    bf16 = jnp.bfloat16
    anywhere = pl.BlockSpec(memory_space=pl.ANY)
    hbm = pl.BlockSpec(memory_space=pltpu.HBM)
    slots = jnp.transpose(page_slot, (0, 2, 1))
    dma = pltpu.SemaphoreType.DMA
    scalars = [
        pltpu.SMEM(prefix_pages.shape, jnp.int32),
        pltpu.SMEM(owner_start.shape, jnp.int32),
        pltpu.SMEM(slots.shape, jnp.int32),
    ]
    numbers = [
        pltpu.with_memory_space_constraint(operand, pltpu.HBM)
        for operand in (prefix_pages, owner_start, slots)
    ]
    arrays = [
        pltpu.with_memory_space_constraint(operand, pltpu.HBM)
        for operand in (queries, suffix_kv.reshape(own_shape), pool_kv)
    ]
    mixed, fresh, pool = pl.pallas_call(
        functools.partial(exchange, groups, prefix_levels),
        out_shape=(
            pltpu.VMEM(queries.shape, bf16),
            pltpu.VMEM((groups,) + page_shape, bf16),
            pltpu.VMEM(pool_kv.shape, bf16),
        ),
        in_specs=[hbm] * 6,
        out_specs=(vmem, vmem, vmem),
        scratch_shapes=scalars
        + [
            pltpu.VMEM(queries.shape, bf16),
            pltpu.VMEM(own_shape, bf16),
            pltpu.VMEM(pool_kv.shape[1:], bf16),
            pltpu.VMEM((prefix_levels * (groups - 1),) + page_shape, bf16),
            pltpu.VMEM((pages,) + page_shape, bf16),
            pltpu.VMEM((groups - 1,) + page_shape, bf16),
            pltpu.VMEM((local_heads, suffix, 2 * dim), bf16),
            pltpu.VMEM((local_heads, pages * page_len, dim), bf16),
            pltpu.VMEM((local_heads, pages * page_len, 2 * dim), bf16),
            pltpu.VMEM((2, heads, suffix, 2 * dim), jnp.float32),
            pltpu.VMEM((2, heads, suffix, dim), jnp.float32),
            dma((6 + 2 * local_heads,)),
            dma((prefix_levels * (groups - 1),)),
            dma((pages,)),
            dma((groups - 1,)),
            dma((groups,)),
            pltpu.SemaphoreType.REGULAR,
        ],
        compiler_params=pltpu.CompilerParams(
            collective_id=0, has_side_effects=True, vmem_limit_bytes=44 * 1024 * 1024
        ),
    )(*numbers, *arrays)
    return pl.pallas_call(
        functools.partial(finish, groups),
        out_shape=(
            jax.ShapeDtypeStruct(queries.shape, bf16),
            jax.ShapeDtypeStruct(pool_kv.shape, bf16),
        ),
        in_specs=[hbm, hbm, hbm, vmem, vmem, vmem],
        out_specs=(anywhere, anywhere),
        scratch_shapes=scalars + [dma((3,)), dma, dma((slot_count,))],
        compiler_params=pltpu.CompilerParams(vmem_limit_bytes=8 * 1024 * 1024),
    )(*numbers, mixed, fresh, pool)


def solution(mesh):
    in_specs = (
        P(("parts", "pool"), "tp"),
        P(None, "tp", ("parts", "pool"), None),
        P(None, "tp", ("parts", "pool"), None, None),
        P("parts"),
        P("parts"),
        P("parts", None, None),
    )
    out_specs = (P(("parts", "pool"), "tp"), P(None, "tp", ("parts", "pool"), None, None))
    return jax.shard_map(body, mesh=mesh, in_specs=in_specs, out_specs=out_specs, check_vma=False)
```
